512 devices in a mesh: tiles: 128 (over y, z, core), rep: 4 (over x).
Axes of the slice: x: 4, y: 8, z: 8, core: 2. Of those that a mesh axis runs over, the one named last changes fastest.
Arguments:
- dissim: float32 [17408, 128, 128], P(('tiles', 'rep')), may hold values from 0.5 to 4
- tile_map: int32 [17408, 2], P(('tiles', 'rep')), may hold values from -1 to 127, as said below
- owned_blocks: int32 [128], P('tiles'), may hold values from 0 to 127, each once
- start_coords: float32 [128, 3, 128], P('tiles'), may hold values from -6 to 6
Outputs:
- coords: float32 [128, 3, 128], P('tiles')
- stress: float32 [], replicated
The draws below stay inside these ranges and needn't reach their ends.
Inputs may be any that keep to these rules, and one draw needn't show every extreme that they name: `tile_map`: every pair (r, c) with 0 <= r <= c < 128 stands in exactly one row; every other row is (-1, -1); the 34 rows of one device are filled by between 0 and 34 tiles, and one device is full.
All inputs are finite; a program needn't handle non-finite values.
Results may differ from the reference program's by a relative error of at most 0.0003.
Values sent between devices are 32-bit elements; how exact they have to be, the bound alone decides.
A program may use at most 64 MiB of HBM per device.

```python
import jax
import jax.numpy as jnp
import numpy as np
from jax import lax

BLK = 128
ITERS = 3
NB = 128
SLOTS = 34
DEVICES = 512


def draw_tile_map(key, part):
    upper_rows, upper_cols = np.triu_indices(NB)
    pairs = jnp.asarray(np.stack([upper_rows, upper_cols], 1).astype(np.int32))
    triangle = int(upper_rows.shape[0])
    key_shift, key_rank, key_full, key_perm = jax.random.split(jax.random.fold_in(key, 7), 4)
    shifts = jax.random.randint(key_shift, (DEVICES,), 0, SLOTS // 2 + 1)
    ranking = jax.random.permutation(key_rank, DEVICES).astype(jnp.int32)
    full_device = jax.random.randint(key_full, (), 0, DEVICES)
    positions = jnp.arange(SLOTS, dtype=jnp.int32)
    devices = jnp.arange(DEVICES, dtype=jnp.int32)
    levels = positions[None, :] - shifts[:, None]
    scores = levels * DEVICES + ranking[:, None]
    scores = jnp.where(devices[:, None] == full_device, positions[None, :] - 4 * SLOTS * DEVICES, scores)
    ordering = jnp.argsort(scores.reshape(-1), stable=True)
    chosen = ordering[:triangle]
    shuffled = jax.random.permutation(key_perm, triangle)
    result = jnp.full((DEVICES * SLOTS, 2), -1, jnp.int32)
    return result.at[chosen].set(pairs[shuffled])


def block_scale(rng, shape, cuts, low, largest):
    def one(position, parts):
        draws = jax.random.uniform(jax.random.fold_in(jax.random.fold_in(rng, 6), position), (parts,), jnp.float32, low / len(cuts), largest / len(cuts))
        return jnp.repeat(jnp.exp(draws), shape[position] // parts).reshape((-1,) + (1,) * (len(shape) - position - 1))

    level = one(*cuts[0])
    for cut in cuts[1:]:
        level = level * one(*cut)
    return level


def centred(key, extent, width, bound, cuts=(), kind=jnp.bfloat16):
    array = jax.random.normal(key, extent, jnp.float32) * width
    if len(cuts) > 0:
        array = block_scale(key, extent, cuts, -0.22, 0.18) * array
    return jnp.clip(array, min=-bound, max=bound).astype(kind)


def setup_inputs(seed: int = 0) -> dict:
    arg_keys = jax.random.split(jax.random.key(seed), 5)
    dissim = jnp.clip(0.5 + 3.5 * jax.random.uniform(arg_keys[0], (DEVICES * SLOTS, BLK, BLK), jnp.float32) ** block_scale(arg_keys[0], (DEVICES * SLOTS, BLK, BLK), ((0, 512),), -0.2, 0.2), 0.5, 4.0)
    tile_map = draw_tile_map(jax.random.fold_in(arg_keys[4], 71), 0)
    owned_blocks = jax.random.permutation(arg_keys[2], NB).astype(jnp.int32)
    start_coords = centred(arg_keys[3], (NB, 3, BLK), 1.0, 6.0, ((0, 128),), jnp.float32)
    return dict(dissim=dissim, tile_map=tile_map, owned_blocks=owned_blocks, start_coords=start_coords)


distance_floor = 0.25

def tile_terms(coords_all, dissim, tile_map, slot_of):
    row_ids = tile_map[:, 0]
    col_ids = tile_map[:, 1]
    occupied = row_ids >= 0
    row_slot = slot_of[jnp.maximum(row_ids, 0)]
    col_slot = slot_of[jnp.maximum(col_ids, 0)]
    row_points = coords_all[row_slot]
    col_points = coords_all[col_slot]
    tile_width = dissim.shape[1]
    offsets = jnp.arange(tile_width, dtype=jnp.int32)
    above_diag = offsets[:, None] < offsets[None, :]
    kept_mask = occupied[:, None, None] & ((row_ids != col_ids)[:, None, None] | above_diag[None])
    squared = jnp.zeros(dissim.shape, jnp.float32)
    for component in range(3):
        spread = row_points[:, component, :, None] - col_points[:, component, None, :]
        squared = squared + spread * spread
    distance = jnp.sqrt(jnp.maximum(squared, distance_floor))
    ratios = jnp.where(kept_mask, dissim / distance, jnp.float32(0.0))
    misfit = jnp.where(kept_mask, (dissim - distance) ** 2, jnp.float32(0.0))
    stress = jnp.sum(misfit)
    row_total = lax.optimization_barrier(jnp.sum(ratios, axis=2))
    col_total = lax.optimization_barrier(jnp.sum(ratios, axis=1))
    row_terms = row_points * row_total[:, None, :] - jnp.einsum('sij,scj->sci', ratios, col_points, precision=lax.Precision.HIGHEST)
    col_terms = col_points * col_total[:, None, :] - jnp.einsum('sij,sci->scj', ratios, row_points, precision=lax.Precision.HIGHEST)
    block_count = coords_all.shape[0]
    totals = jnp.zeros((block_count, 3, tile_width), jnp.float32)
    totals = totals.at[row_slot].add(row_terms).at[col_slot].add(col_terms)
    return (totals, stress)

def reference(dissim, tile_map, owned_blocks, start_coords):
    block_count = owned_blocks.shape[0]
    slot_of = jnp.zeros((block_count,), jnp.int32).at[owned_blocks].set(jnp.arange(block_count, dtype=jnp.int32))
    tile_width = dissim.shape[1]
    grouped = dissim.reshape(DEVICES, SLOTS, tile_width, tile_width)
    grouped_map = tile_map.reshape(DEVICES, SLOTS, 2)
    coords_all = start_coords
    stress = jnp.float32(0.0)
    for step in range(ITERS):

        def accumulate(carry, pieces):
            totals, misfit = carry
            more, extra = tile_terms(coords_all, pieces[0], pieces[1], slot_of)
            return ((totals + more, misfit + extra), None)
        start = (jnp.zeros(coords_all.shape, jnp.float32), jnp.float32(0.0))
        (totals, stress), unused = lax.scan(accumulate, start, (grouped, grouped_map))
        coords_all = totals / jnp.float32(block_count * tile_width)
    return (coords_all, stress)
```

```python
import functools

import jax
import jax.numpy as jnp
from jax import lax
from jax.experimental import pallas as pl
from jax.experimental.pallas import tpu as pltpu
from jax.sharding import PartitionSpec as P

MESH = pl.DeviceIdType.MESH
F32, BF16 = jnp.float32, jnp.bfloat16
ITERS = 3
FLOOR = 0.25
Q = 24


def pieces(v):
    a = v.astype(BF16)
    rest = v - a.astype(F32)
    b = rest.astype(BF16)
    c = (rest - b.astype(F32)).astype(BF16)
    return a, b, c


def ring_order(n):
    return sorted(range(n), key=lambda d: -min(d, n - d))


def dot(a, b, dims=((1,), (0,))):
    return lax.dot_general(a, b, (dims, ((), ())), preferred_element_type=F32)


def kernel(sizes, dissim, map_v, map_s, owned, start, coords_out, stress_out, *scratch):
    nx, ny, nz, slots, wide = sizes
    (tiles, xs, grid, c_in, half, z_in, y_in, x_in, first, side_a, side_b, sum_a, sum_b, full, hot, hot_t,
     s_core, s_z, s_y, s_x, load_sem,
     f_send, f_recv, cs, cr, zs, zr, ys, yr, xsd, xrv, ags, agr, acs, acr,
     scs, scr, szs, szr, sys_, syr, sxs, sxr) = scratch
    pad = side_a.shape[0]
    blk = 128
    count = 2 * nz * ny
    t = lax.axis_index("tiles")
    x = lax.axis_index("rep")
    y = t // (2 * nz)
    z = (t // 2) % nz
    core = t % 2
    mine = core * nz + z

    def at(x_, y_, z_, c_):
        return {"tiles": (y_ * nz + z_) * 2 + c_, "rep": x_}

    partner = at(x, y, z, 1 - core)

    def z_peer(d):
        return at(x, y, (z + d) % nz, core)

    def y_peer(d):
        return at(x, (y + d) % ny, z, core)

    def x_peer(d):
        return at((x + d) % nx, y, z, core)

    def send(src, dst, send_sem, recv_sem, peer):
        copy = pltpu.make_async_remote_copy(
            src_ref=src, dst_ref=dst, send_sem=send_sem, recv_sem=recv_sem, device_id=peer, device_id_type=MESH
        )
        copy.start()
        return copy

    z_far, y_far, x_far = ring_order(nz), ring_order(ny), ring_order(nx)

    load = pltpu.make_async_copy(dissim, tiles, load_sem)
    load.start()

    barrier = pltpu.get_barrier_semaphore()
    peers = [partner] + [z_peer(d) for d in range(1, nz)]
    peers += [y_peer(d) for d in range(1, ny)] + [x_peer(d) for d in range(1, nx)]
    for peer in peers:
        pl.semaphore_signal(barrier, inc=1, device_id=peer, device_id_type=MESH)

    first[y, pl.ds(0, 3), :] = start[0]
    first[y, pl.ds(3, 1), :] = jnp.full((1, blk), owned[0].astype(F32))
    first[y, pl.ds(4, 4), :] = jnp.zeros((4, blk), F32)
    pl.semaphore_wait(barrier, len(peers))

    sends = [send(first.at[y], first.at[y], f_send.at[d], f_recv.at[d], y_peer(d)) for d in y_far if d]

    ones = jnp.ones((pad, blk), F32)
    for q in range(18, 21):
        side_b[:, q, :] = ones
        side_a[:, q + 3, :] = ones
    for s in range(slots, pad):
        sum_a[s] = jnp.zeros((Q, blk), F32)
        sum_b[s] = jnp.zeros((Q, blk), F32)
    hot[...] = jnp.zeros((2 * pad, count), F32)

    load.wait()
    above = lax.broadcasted_iota(jnp.int32, (blk, blk), 0) < lax.broadcasted_iota(jnp.int32, (blk, blk), 1)

    def drop(s, carry):
        row, col = map_s[s, 0], map_s[s, 1]
        occupied = row >= 0
        upper = jnp.where(occupied, F32(1), F32(0))
        lower = jnp.where(occupied & (row != col), F32(1), F32(0))
        tiles[s] = tiles[s] * jnp.where(above, upper, lower)
        return carry

    lax.fori_loop(0, slots, drop, 0)

    for copy in sends:
        copy.wait_recv()
    for c in range(4):
        xs[mine, c] = first[:, c, :]
    for copy in sends:
        copy.wait_send()

    def gather_all(planes):
        own = xs.at[mine, pl.ds(0, planes)]
        out = [send(own, own, ags.at[d], agr.at[d], z_peer(d)) for d in z_far if d]
        across = {0: send(own, own, acs.at[0], acr.at[0], partner)}
        for copy, d in reversed(list(zip(out, [d for d in z_far if d]))):
            copy.wait_recv()
            came = xs.at[core * nz + (z - d + nz) % nz, pl.ds(0, planes)]
            across[d] = send(came, came, acs.at[d], acr.at[d], partner)
        for copy in across.values():
            copy.wait_recv()
        for copy in out + list(across.values()):
            copy.wait_send()

    gather_all(4)

    order = xs[:, 3].reshape(count, blk)
    order_row = jnp.transpose(order)
    ids = map_v[...].astype(F32)
    hot[pl.ds(0, slots), :] = jnp.where(ids[:, 0:1] == order_row[0:1], F32(1), F32(0))
    hot[pl.ds(pad, slots), :] = jnp.where(ids[:, 1:2] == order_row[0:1], F32(1), F32(0))
    hot_t[...] = jnp.transpose(hot[...])

    for step in range(ITERS):
        last = step == ITERS - 1

        pick = hot[...].astype(BF16)
        norm = jnp.zeros((2 * pad, blk), F32)
        for c in range(3):
            parts = [dot(pick, v) for v in pieces(xs[:, c].reshape(count, blk))]
            value = parts[0] + parts[1] + parts[2]
            full[c] = value
            norm = norm + value * value
            for q, (a, b) in enumerate(((0, 0), (0, 1), (1, 0), (1, 1), (0, 2), (2, 0))):
                side_a[:, 6 * c + q, :] = parts[a][:pad]
                side_b[:, 6 * c + q, :] = -2.0 * parts[b][pad:]
        for q, v in enumerate(pieces(norm)):
            side_a[:, 18 + q, :] = v.astype(F32)[:pad]
            side_b[:, 21 + q, :] = v.astype(F32)[pad:]

        def tile(s, stress):
            a = side_a[s].astype(BF16)
            b = side_b[s].astype(BF16)
            squared = jnp.maximum(dot(a, b, ((0,), (0,))), FLOOR)
            inverse = lax.rsqrt(squared)
            delta = tiles[s]
            ratio = delta * inverse
            high = ratio.astype(BF16)
            low = (ratio - high.astype(F32)).astype(BF16)
            sum_a[s] = dot(a, high) + dot(a, low)
            sum_b[s] = dot(b, high, ((1,), (1,))) + dot(b, low, ((1,), (1,)))
            if last:
                misfit = jnp.where(delta > 0.0, delta - squared * inverse, F32(0))
                stress = stress + jnp.sum((misfit * misfit).reshape(blk // 8, 8, blk), axis=0)
            return stress

        stress = lax.fori_loop(0, slots, tile, jnp.zeros((8, blk), F32))

        drop_t = hot_t[...].astype(BF16)
        row_total, col_total = sum_b[:, 18, :], sum_a[:, 21, :]
        for c in range(3):
            row_sum = -0.5 * (sum_b[:, 6 * c, :] + sum_b[:, 6 * c + 1, :] + sum_b[:, 6 * c + 4, :])
            col_sum = sum_a[:, 6 * c, :] + sum_a[:, 6 * c + 2, :] + sum_a[:, 6 * c + 5, :]
            points = full[c]
            terms = jnp.concatenate([points[:pad] * row_total - row_sum, points[pad:] * col_total - col_sum], axis=0)
            total = functools.reduce(jnp.add, [dot(drop_t, v) for v in pieces(terms)])
            grid[:, c] = total.reshape(2 * nz, ny, blk)

        crossing = {}
        for d in z_far:
            to = (z + d) % nz
            crossing[d] = send(grid.at[(1 - core) * nz + to], c_in.at[to], cs.at[d], cr.at[d], partner)
        waits = list(crossing.values())
        if last:
            s_core[core] = jnp.sum(stress, axis=0, keepdims=True)
            small = send(s_core.at[core], s_core.at[core], scs, scr, partner)
            waits.append(small)
        along = []
        for d in z_far:
            to = (z + d) % nz
            crossing[d].wait_recv()
            if d:
                half[to] = grid[core * nz + to] + c_in[to]
                along.append(send(half.at[to], z_in.at[z], zs.at[d], zr.at[d], z_peer(d)))
            else:
                z_in[z] = grid[mine] + c_in[z]
        if last:
            small.wait_recv()
            s_z[z] = s_core[0] + s_core[1]
            along += [send(s_z.at[z], s_z.at[z], szs.at[d], szr.at[d], z_peer(d)) for d in z_far if d]
        for copy in along:
            copy.wait_recv()
        waits += along

        y_in[step, y] = functools.reduce(jnp.add, [z_in[k] for k in range(nz)])
        own = y_in.at[step, y]
        along = [send(own, own, ys.at[step, d], yr.at[step, d], y_peer(d)) for d in y_far if d]
        if last:
            s_y[y] = functools.reduce(jnp.add, [s_z[k] for k in range(nz)])
            along += [send(s_y.at[y], s_y.at[y], sys_.at[d], syr.at[d], y_peer(d)) for d in y_far if d]
        for copy in along:
            copy.wait_recv()
        waits += along

        x_in[step, x] = functools.reduce(jnp.add, [y_in[step, k] for k in range(ny)])
        own = x_in.at[step, x]
        along = [send(own, own, xsd.at[step, d], xrv.at[step, d], x_peer(d)) for d in x_far if d]
        if last:
            s_x[x] = functools.reduce(jnp.add, [s_y[k] for k in range(ny)])
            along += [send(s_x.at[x], s_x.at[x], sxs.at[d], sxr.at[d], x_peer(d)) for d in x_far if d]
        for copy in along:
            copy.wait_recv()
        waits += along

        if last:
            for c in range(3):
                rows = functools.reduce(jnp.add, [x_in[step, k, c, pl.ds(y, 1), :] for k in range(nx)])
                coords_out[0, pl.ds(c, 1), :] = rows * F32(1.0 / (count * blk))
            stress_out[0, 0] = jnp.sum(functools.reduce(jnp.add, [s_x[k] for k in range(nx)]))
        else:
            piece = functools.reduce(jnp.add, [x_in[step, k] for k in range(nx)])
            xs[mine, pl.ds(0, 3)] = piece * F32(1.0 / (count * blk))
            gather_all(3)
        for copy in waits:
            copy.wait_send()


def local(sizes, dissim, tile_map, owned_blocks, start_coords):
    nx, ny, nz, slots, wide = sizes
    blk = dissim.shape[1]
    pad = -(-slots // 8) * 8
    count = 2 * nz * ny
    dma = pltpu.SemaphoreType.DMA
    vmem = lambda *shape: pltpu.VMEM(shape, F32)
    coords, stress = pl.pallas_call(
        functools.partial(kernel, sizes),
        out_shape=(
            jax.ShapeDtypeStruct((1, 3, blk), F32),
            jax.ShapeDtypeStruct((1, 1), F32),
        ),
        in_specs=[
            pl.BlockSpec(memory_space=pl.ANY),
            pl.BlockSpec(memory_space=pltpu.VMEM),
            pl.BlockSpec(memory_space=pltpu.SMEM),
            pl.BlockSpec(memory_space=pltpu.SMEM),
            pl.BlockSpec(memory_space=pltpu.VMEM),
        ],
        out_specs=(
            pl.BlockSpec(memory_space=pltpu.VMEM),
            pl.BlockSpec(memory_space=pltpu.SMEM),
        ),
        scratch_shapes=[
            vmem(slots, blk, blk),
            vmem(2 * nz, 4, ny, blk),
            vmem(2 * nz, 3, ny, blk),
            vmem(nz, 3, ny, blk),
            vmem(nz, 3, ny, blk),
            vmem(nz, 3, ny, blk),
            vmem(ITERS, ny, 3, ny, blk),
            vmem(ITERS, nx, 3, ny, blk),
            vmem(ny, 8, blk),
            vmem(pad, Q, blk),
            vmem(pad, Q, blk),
            vmem(pad, Q, blk),
            vmem(pad, Q, blk),
            vmem(3, 2 * pad, blk),
            vmem(2 * pad, count),
            vmem(count, 2 * pad),
            vmem(2, 1, blk),
            vmem(nz, 1, blk),
            vmem(ny, 1, blk),
            vmem(nx, 1, blk),
            dma,
            dma((ny,)), dma((ny,)),
            dma((nz,)), dma((nz,)),
            dma((nz,)), dma((nz,)),
            dma((ITERS, ny)), dma((ITERS, ny)),
            dma((ITERS, nx)), dma((ITERS, nx)),
            dma((nz,)), dma((nz,)),
            dma((nz,)), dma((nz,)),
            dma, dma,
            dma((nz,)), dma((nz,)),
            dma((ny,)), dma((ny,)),
            dma((nx,)), dma((nx,)),
        ],
        compiler_params=pltpu.CompilerParams(
            collective_id=0, has_side_effects=True, vmem_limit_bytes=32 * 2**20
        ),
        name="guttman",
    )(dissim, tile_map, tile_map, owned_blocks, start_coords)
    return coords, stress.reshape(())


def build(mesh, ny, nz, slots):
    nx = mesh.shape["rep"]
    sizes = (nx, ny, nz, slots, 0)
    both = ("tiles", "rep")
    return jax.shard_map(
        functools.partial(local, sizes),
        mesh=mesh,
        in_specs=(P(both, None, None), P(both, None), P("tiles"), P("tiles", None, None)),
        out_specs=(P("tiles", None, None), P()),
        check_vma=False,
    )


def solution(mesh):
    return build(mesh, 8, 8, 34)
```

```python
import functools

import jax
import jax.numpy as jnp
from jax import lax
from jax.experimental import pallas as pl
from jax.experimental.pallas import tpu as pltpu
from jax.sharding import PartitionSpec as P

MESH = pl.DeviceIdType.MESH
F32, BF16 = jnp.float32, jnp.bfloat16
ITERS = 3
FLOOR = 0.25
Q = 24


def pieces(v):
    a = v.astype(BF16)
    rest = v - a.astype(F32)
    b = rest.astype(BF16)
    c = (rest - b.astype(F32)).astype(BF16)
    return a, b, c


def ring_order(n):
    return sorted(range(n), key=lambda d: -min(d, n - d))


def dot(a, b, dims=((1,), (0,))):
    return lax.dot_general(a, b, (dims, ((), ())), preferred_element_type=F32)


def kernel(sizes, dissim, map_v, map_s, owned, start, coords_out, stress_out, *scratch):
    nx, ny, nz, slots, unroll = sizes
    (tiles, tiles_t, xs, grid, c_in, half, z_in, y_in, x_in, first, side_a, side_b, sum_a, sum_b, full, hot_r, hot_c,
     s_core, s_z, s_y, s_x, load_sem,
     f_send, f_recv, cs, cr, zs, zr, ys, yr, xsd, xrv, ags, agr, acs, acr,
     scs, scr, szs, szr, sys_, syr, sxs, sxr) = scratch
    pad = side_a.shape[0]
    blk = 128
    count = 2 * nz * ny
    t = lax.axis_index("tiles")
    x = lax.axis_index("rep")
    y = t // (2 * nz)
    z = (t // 2) % nz
    core = t % 2
    mine = core * nz + z

    def at(x_, y_, z_, c_):
        return {"tiles": (y_ * nz + z_) * 2 + c_, "rep": x_}

    partner = at(x, y, z, 1 - core)

    def z_peer(d):
        return at(x, y, (z + d) % nz, core)

    def y_peer(d):
        return at(x, (y + d) % ny, z, core)

    def x_peer(d):
        return at((x + d) % nx, y, z, core)

    def send(src, dst, send_sem, recv_sem, peer):
        copy = pltpu.make_async_remote_copy(
            src_ref=src, dst_ref=dst, send_sem=send_sem, recv_sem=recv_sem, device_id=peer, device_id_type=MESH
        )
        copy.start()
        return copy

    z_far, y_far, x_far = ring_order(nz), ring_order(ny), ring_order(nx)

    load = pltpu.make_async_copy(dissim, tiles, load_sem)
    load.start()

    barrier = pltpu.get_barrier_semaphore()
    peers = [partner] + [z_peer(d) for d in range(1, nz)]
    peers += [y_peer(d) for d in range(1, ny)] + [x_peer(d) for d in range(1, nx)]
    for peer in peers:
        pl.semaphore_signal(barrier, inc=1, device_id=peer, device_id_type=MESH)

    for c in range(3):
        first[y, pl.ds(c, 1), :] = start[c]
    first[y, pl.ds(3, 1), :] = jnp.full((1, blk), owned[0].astype(F32))
    first[y, pl.ds(4, 4), :] = jnp.zeros((4, blk), F32)
    pl.semaphore_wait(barrier, len(peers))

    sends = [send(first.at[y], first.at[y], f_send.at[d], f_recv.at[d], y_peer(d)) for d in y_far if d]

    ones = jnp.ones((pad, blk), F32)
    for q in range(18, 21):
        side_b[:, q, :] = ones
        side_a[:, q + 3, :] = ones
    for s in range(slots, pad):
        sum_a[s] = jnp.zeros((Q, blk), F32)
        sum_b[s] = jnp.zeros((Q, blk), F32)
    hot_r[...] = jnp.zeros((count, blk), F32)
    hot_c[...] = jnp.zeros((count, blk), F32)

    load.wait()
    above = lax.broadcasted_iota(jnp.int32, (blk, blk), 0) < lax.broadcasted_iota(jnp.int32, (blk, blk), 1)

    def drop(s, carry):
        row, col = map_s[0, s], map_s[1, s]
        occupied = row >= 0
        upper = jnp.where(occupied, F32(1), F32(0))
        lower = jnp.where(occupied & (row != col), F32(1), F32(0))
        kept = tiles[s] * jnp.where(above, upper, lower)
        tiles[s] = kept
        tiles_t[s] = jnp.transpose(kept)
        return carry

    lax.fori_loop(0, slots, drop, 0, unroll=2)

    for copy in sends:
        copy.wait_recv()
    for c in range(4):
        xs[mine, c] = first[:, c, :]
    for copy in sends:
        copy.wait_send()

    def gather_all(planes):
        own = xs.at[mine, pl.ds(0, planes)]
        out = [send(own, own, ags.at[d], agr.at[d], z_peer(d)) for d in z_far if d]
        across = {0: send(own, own, acs.at[0], acr.at[0], partner)}
        for copy, d in reversed(list(zip(out, [d for d in z_far if d]))):
            copy.wait_recv()
            came = xs.at[core * nz + (z - d + nz) % nz, pl.ds(0, planes)]
            across[d] = send(came, came, acs.at[d], acr.at[d], partner)
        for copy in across.values():
            copy.wait_recv()
        for copy in out + list(across.values()):
            copy.wait_send()

    gather_all(4)

    order = xs[:, 3].reshape(count, blk)[:, :slots]
    ids = map_v[...].astype(F32)
    hot_r[:, pl.ds(0, slots)] = jnp.where(order == ids[0:1], F32(1), F32(0))
    hot_c[:, pl.ds(0, slots)] = jnp.where(order == ids[1:2], F32(1), F32(0))
    pick = jnp.concatenate([jnp.transpose(hot_r[...])[:pad], jnp.transpose(hot_c[...])[:pad]], axis=0).astype(BF16)
    put = jnp.concatenate([hot_r[...], hot_c[...]], axis=1).astype(BF16)

    for step in range(ITERS):
        last = step == ITERS - 1

        norm = jnp.zeros((2 * pad, blk), F32)
        for c in range(3):
            parts = [dot(pick, v) for v in pieces(xs[:, c].reshape(count, blk))]
            value = parts[0] + parts[1] + parts[2]
            full[c] = value
            norm = norm + value * value
            for q, (a, b) in enumerate(((0, 0), (0, 1), (1, 0), (1, 1), (0, 2), (2, 0))):
                side_a[:, 6 * c + q, :] = parts[a][:pad]
                side_b[:, 6 * c + q, :] = -2.0 * parts[b][pad:]
        for q, v in enumerate(pieces(norm)):
            side_a[:, 18 + q, :] = v.astype(F32)[:pad]
            side_b[:, 21 + q, :] = v.astype(F32)[pad:]

        def tile(s, stress):
            a = side_a[s].astype(BF16)
            b = side_b[s].astype(BF16)
            for near, far, deltas, sums in ((a, b, tiles, sum_a), (b, a, tiles_t, sum_b)):
                squared = jnp.maximum(dot(near, far, ((0,), (0,))), FLOOR)
                inverse = lax.rsqrt(squared)
                delta = deltas[s]
                ratio = delta * inverse
                high = ratio.astype(BF16)
                low = (ratio - high.astype(F32)).astype(BF16)
                sums[s] = dot(jnp.concatenate([near, near], axis=1), jnp.concatenate([high, low], axis=0))
                if last and deltas is tiles:
                    misfit = jnp.where(delta > 0.0, delta - squared * inverse, F32(0))
                    stress = stress + jnp.sum((misfit * misfit).reshape(blk // 8, 8, blk), axis=0)
            return stress

        stress = lax.fori_loop(0, slots, tile, jnp.zeros((8, blk), F32), unroll=unroll)

        row_total, col_total = sum_b[:, 18, :], sum_a[:, 21, :]
        for c in range(3):
            row_sum = -0.5 * (sum_b[:, 6 * c, :] + sum_b[:, 6 * c + 1, :] + sum_b[:, 6 * c + 4, :])
            col_sum = sum_a[:, 6 * c, :] + sum_a[:, 6 * c + 2, :] + sum_a[:, 6 * c + 5, :]
            points = full[c]
            spare = jnp.zeros((blk - pad, blk), F32)
            row_terms = jnp.concatenate([points[:pad] * row_total - row_sum, spare], axis=0)
            col_terms = jnp.concatenate([points[pad:] * col_total - col_sum, spare], axis=0)
            terms = jnp.concatenate([row_terms, col_terms], axis=0)
            total = functools.reduce(jnp.add, [dot(put, v) for v in pieces(terms)])
            grid[:, c] = total.reshape(2 * nz, ny, blk)

        crossing = {}
        for d in z_far:
            to = (z + d) % nz
            crossing[d] = send(grid.at[(1 - core) * nz + to], c_in.at[to], cs.at[d], cr.at[d], partner)
        waits = list(crossing.values())
        if last:
            s_core[core] = jnp.sum(stress, axis=0, keepdims=True)
            small = send(s_core.at[core], s_core.at[core], scs, scr, partner)
            waits.append(small)
        along = []
        for d in z_far:
            to = (z + d) % nz
            crossing[d].wait_recv()
            if d:
                half[to] = grid[core * nz + to] + c_in[to]
                along.append(send(half.at[to], z_in.at[z], zs.at[d], zr.at[d], z_peer(d)))
            else:
                z_in[z] = grid[mine] + c_in[z]
        if last:
            small.wait_recv()
            s_z[z] = s_core[0] + s_core[1]
            along += [send(s_z.at[z], s_z.at[z], szs.at[d], szr.at[d], z_peer(d)) for d in z_far if d]
        for copy in along:
            copy.wait_recv()
        waits += along

        y_in[step, y] = functools.reduce(jnp.add, [z_in[k] for k in range(nz)])
        own = y_in.at[step, y]
        along = [send(own, own, ys.at[step, d], yr.at[step, d], y_peer(d)) for d in y_far if d]
        if last:
            s_y[y] = functools.reduce(jnp.add, [s_z[k] for k in range(nz)])
            along += [send(s_y.at[y], s_y.at[y], sys_.at[d], syr.at[d], y_peer(d)) for d in y_far if d]
        for copy in along:
            copy.wait_recv()
        waits += along

        x_in[step, x] = functools.reduce(jnp.add, [y_in[step, k] for k in range(ny)])
        own = x_in.at[step, x]
        along = [send(own, own, xsd.at[step, d], xrv.at[step, d], x_peer(d)) for d in x_far if d]
        if last:
            s_x[x] = functools.reduce(jnp.add, [s_y[k] for k in range(ny)])
            along += [send(s_x.at[x], s_x.at[x], sxs.at[d], sxr.at[d], x_peer(d)) for d in x_far if d]
        for copy in along:
            copy.wait_recv()
        waits += along

        if last:
            for c in range(3):
                rows = functools.reduce(jnp.add, [x_in[step, k, c, pl.ds(y, 1), :] for k in range(nx)])
                coords_out[c] = rows * F32(1.0 / (count * blk))
            stress_out[0, 0] = jnp.sum(functools.reduce(jnp.add, [s_x[k] for k in range(nx)]))
        else:
            piece = functools.reduce(jnp.add, [x_in[step, k] for k in range(nx)])
            xs[mine, pl.ds(0, 3)] = piece * F32(1.0 / (count * blk))
            gather_all(3)
        for copy in waits:
            copy.wait_send()


def local(sizes, dissim, tile_map, owned_blocks, start_coords):
    nx, ny, nz, slots, unroll = sizes
    blk = dissim.shape[1]
    pad = -(-slots // 8) * 8
    count = 2 * nz * ny
    dma = pltpu.SemaphoreType.DMA
    vmem = lambda *shape: pltpu.VMEM(shape, F32)
    coords, stress = pl.pallas_call(
        functools.partial(kernel, sizes),
        out_shape=(
            jax.ShapeDtypeStruct((3, 1, blk), F32),
            jax.ShapeDtypeStruct((1, 1), F32),
        ),
        in_specs=[
            pl.BlockSpec(memory_space=pltpu.HBM),
            pl.BlockSpec(memory_space=pltpu.VMEM),
            pl.BlockSpec(memory_space=pltpu.SMEM),
            pl.BlockSpec(memory_space=pltpu.SMEM),
            pl.BlockSpec(memory_space=pltpu.VMEM),
        ],
        out_specs=(
            pl.BlockSpec(memory_space=pltpu.VMEM),
            pl.BlockSpec(memory_space=pltpu.SMEM),
        ),
        scratch_shapes=[
            vmem(slots, blk, blk),
            vmem(slots, blk, blk),
            vmem(2 * nz, 4, ny, blk),
            vmem(2 * nz, 3, ny, blk),
            vmem(nz, 3, ny, blk),
            vmem(nz, 3, ny, blk),
            vmem(nz, 3, ny, blk),
            vmem(ITERS, ny, 3, ny, blk),
            vmem(ITERS, nx, 3, ny, blk),
            vmem(ny, 8, blk),
            vmem(pad, Q, blk),
            vmem(pad, Q, blk),
            vmem(pad, Q, blk),
            vmem(pad, Q, blk),
            vmem(3, 2 * pad, blk),
            vmem(count, blk),
            vmem(count, blk),
            vmem(2, 1, blk),
            vmem(nz, 1, blk),
            vmem(ny, 1, blk),
            vmem(nx, 1, blk),
            dma,
            dma((ny,)), dma((ny,)),
            dma((nz,)), dma((nz,)),
            dma((nz,)), dma((nz,)),
            dma((ITERS, ny)), dma((ITERS, ny)),
            dma((ITERS, nx)), dma((ITERS, nx)),
            dma((nz,)), dma((nz,)),
            dma((nz,)), dma((nz,)),
            dma, dma,
            dma((nz,)), dma((nz,)),
            dma((ny,)), dma((ny,)),
            dma((nx,)), dma((nx,)),
        ],
        compiler_params=pltpu.CompilerParams(
            collective_id=0, has_side_effects=True, vmem_limit_bytes=63 * 2**20
        ),
        name="guttman",
    )(dissim, tile_map.T, tile_map.T, owned_blocks, jnp.swapaxes(start_coords, 0, 1))
    return jnp.swapaxes(coords, 0, 1), stress.reshape(())


def build(mesh, ny, nz, slots):
    nx = mesh.shape["rep"]
    sizes = (nx, ny, nz, slots, next(u for u in (17, 7, 5, 3, 2, 1) if slots % u == 0))
    both = ("tiles", "rep")
    return jax.shard_map(
        functools.partial(local, sizes),
        mesh=mesh,
        in_specs=(P(both, None, None), P(both, None), P("tiles"), P("tiles", None, None)),
        out_specs=(P("tiles", None, None), P()),
        check_vma=False,
    )


def solution(mesh):
    return build(mesh, 8, 8, 34)
```
